32 devices in a mesh: sens: 4 (over y, core), par: 8 (over z, x).
Axes of the slice: x: 2, y: 2, z: 4, core: 2. Of those that a mesh axis runs over, the one named last changes fastest.
Arguments:
- probes: float32 [2048, 512], P('par', 'sens'), may hold values from -6 to 6
- kernel: float32 [64, 2048, 2048], P(None, 'par', 'sens'), may hold values from -0.015625 to 0.015625
- noise_inverse: float32 [64, 64], replicated, may hold values from -1 to 3, as said below
- sensor_weight: float32 [2048], P('sens'), may hold values from 0.25 to 4
Outputs:
- hessian_action: float32 [2048, 512], P('par', 'sens')
The draws below stay inside these ranges and needn't reach their ends.
Inputs may be any that keep to these rules, and one draw needn't show every extreme that they name: `noise_inverse`: symmetric.
All inputs are finite; a program needn't handle non-finite values.
Results may differ from the reference program's by a relative error of at most 0.0001.
Values sent between devices are 32-bit elements; how exact they have to be, the bound alone decides.
A program may use at most 192 MiB of HBM per device.

```python
import math
import jax
import jax.numpy as jnp
from jax import lax

NS = 2048
NP = 2048
NT = 64
PROBES = 8


def draw_noise_inverse(key, part):
    first, second = jax.random.split(jax.random.fold_in(key, 17))
    offdiag = jnp.clip(jax.random.normal(first, (NT, NT), jnp.float32), -4.0, 4.0)
    offdiag = (offdiag + offdiag.T) * (0.12 / NT ** 0.5)
    diagonal = jax.random.uniform(second, (NT,), jnp.float32, 1.0, 2.0)
    return offdiag + jnp.diag(diagonal)


def level_of(stream_key, shape, cuts, low, top_value):
    loudness = 1.0
    for dim, parts in cuts:
        heights = jax.random.uniform(jax.random.fold_in(jax.random.fold_in(stream_key, 6), dim), (parts,), jnp.float32, low / len(cuts), top_value / len(cuts))
        loudness = loudness * jnp.repeat(jnp.exp(heights), shape[dim] // parts).reshape((-1,) + (1,) * (len(shape) - 1 - dim))
    return loudness


def normal_values(rng, dims, deviation, limit, cuts=(), kind=jnp.bfloat16):
    values = jax.random.normal(rng, dims, jnp.float32) * deviation
    if len(cuts) > 0:
        values = level_of(rng, dims, cuts, -0.22, 0.18) * values
    return jnp.clip(values, min=-limit, max=limit).astype(kind)


def setup_inputs(seed: int = 0) -> dict:
    streams_of = jax.random.split(jax.random.key(seed), 5)
    probes = normal_values(streams_of[0], (NP, NT * PROBES), 1.0, 6.0, ((0, 8), (1, 4)), jnp.float32)
    kernel = normal_values(streams_of[1], (NT, NP, NS), (NP * NT) ** -0.5, 0.015625, ((1, 8), (2, 4)), jnp.float32)
    noise_inverse = draw_noise_inverse(jax.random.fold_in(streams_of[4], 71), 0)
    sensor_weight = jnp.clip(jnp.exp(math.log(4.0) - 2.7725887 * jax.random.uniform(streams_of[3], (NS,), jnp.float32) ** level_of(streams_of[3], (NS,), ((0, 4),), -0.2, 0.2)), 0.25, 4.0)
    return dict(probes=probes, kernel=kernel, noise_inverse=noise_inverse, sensor_weight=sensor_weight)


def shift_later(field, lag_index):
    padded = jnp.pad(field, ((0, 0), (NT, 0), (0, 0)))
    return lax.dynamic_slice_in_dim(padded, NT - lag_index, NT, 1)


def shift_earlier(field, lag_index):
    padded = jnp.pad(field, ((0, 0), (0, NT), (0, 0)))
    return lax.dynamic_slice_in_dim(padded, lag_index, NT, 1)


def reference(probes, kernel, noise_inverse, sensor_weight):
    highest = lax.Precision.HIGHEST
    probe_field = probes.reshape(NP, NT, PROBES)
    lag_list = jnp.arange(NT, dtype=jnp.int32)

    def forward(running, lag_index):
        kernel_lag = lax.dynamic_index_in_dim(kernel, lag_index, 0, keepdims=False)
        moved = shift_later(probe_field, lag_index).reshape(NP, NT * PROBES)
        term = lax.dot_general(kernel_lag, moved, (((0,), (0,)), ((), ())), precision=highest, preferred_element_type=jnp.float32)
        return running + term, None

    observed, _ = lax.scan(forward, jnp.zeros((NS, NT * PROBES), jnp.float32), lag_list)
    mixed = jnp.einsum("tu,rup->rtp", noise_inverse, observed.reshape(NS, NT, PROBES), precision=highest, preferred_element_type=jnp.float32)
    weighted = mixed.reshape(NS, NT * PROBES) * sensor_weight[:, None]

    def backward(running, lag_index):
        kernel_lag = lax.dynamic_index_in_dim(kernel, lag_index, 0, keepdims=False)
        spread = jnp.dot(kernel_lag, weighted, precision=highest, preferred_element_type=jnp.float32).reshape(NP, NT, PROBES)
        return running + shift_earlier(spread, lag_index), None

    result, _ = lax.scan(backward, jnp.zeros((NP, NT, PROBES), jnp.float32), lag_list)
    return result.reshape(NP, NT * PROBES)
```

```python
import functools

import jax
import jax.numpy as jnp
from jax import lax
from jax.experimental import pallas as pl
from jax.experimental.pallas import tpu as pltpu
from jax.sharding import PartitionSpec as P

MESH = pl.DeviceIdType.MESH
LAGS = 4
SLOTS = 8
F32 = jnp.float32
BF16 = jnp.bfloat16


def split(value):
    high = value.astype(BF16)
    return high, (value - high.astype(F32)).astype(BF16)


def dot3(left, right, transposed=False):
    dims = (((1,), (1 if transposed else 0,)), ((), ()))
    (lh, ll), (rh, rl) = left, right
    mul = functools.partial(lax.dot_general, dimension_numbers=dims, preferred_element_type=F32)
    return mul(lh, rh) + mul(ll, rh) + mul(lh, rl)


def kernel_body(
    n_sens, n_par, chunks,
    probes, kern, noise, weight, out,
    gath, field, fe_h, fe_l, fo_h, fo_l, stage, k_h, k_l,
    obs, rs_buf, full, we_h, we_l, wo_h, wo_l, mix_h, mix_l, acc, fin,
    k_sem, g_send, g_recv, rs_send, rs_recv, ag_send, ag_recv, f_send, f_recv,
):
    steps, par_rows, sensors = kern.shape
    columns = acc.shape[0]
    p_count = columns // steps
    width = sensors // chunks
    groups = steps // LAGS
    span = LAGS * p_count
    own_cols = probes.shape[1]
    piece = columns // n_par
    par, sens = lax.axis_index("par"), lax.axis_index("sens")

    def fetch(chunk, group, slot):
        return pltpu.make_async_copy(
            kern.at[pl.ds(group * LAGS, LAGS), :, pl.ds(pl.multiple_of(chunk * width, width), width)],
            stage.at[slot], k_sem.at[slot])

    for n in range(SLOTS):
        fetch(n // groups, n % groups, n % SLOTS).start()

    barrier = pltpu.get_barrier_semaphore()
    for k in range(1, n_par):
        pl.semaphore_signal(barrier, inc=1, device_id={"par": lax.rem(par + k, n_par)}, device_id_type=MESH)
    for k in range(1, n_sens):
        pl.semaphore_signal(barrier, inc=1, device_id={"sens": lax.rem(sens + k, n_sens)}, device_id_type=MESH)
    pl.semaphore_wait(barrier, n_par + n_sens - 2)

    gathers = [
        pltpu.make_async_remote_copy(
            src_ref=probes, dst_ref=gath.at[sens], send_sem=g_send.at[k], recv_sem=g_recv.at[k],
            device_id={"sens": lax.rem(sens + k, n_sens)}, device_id_type=MESH)
        for k in range(1, n_sens)
    ]
    for copy in gathers:
        copy.start()
    gath[sens] = probes[...]

    def split_lag(slot, i, lag, chunk):
        high, low = split(stage[slot, i])
        rows = pl.ds(pl.multiple_of(lag * par_rows, par_rows), par_rows)
        cols = pl.ds(chunk * width, width)
        k_h[rows, cols] = high
        k_l[rows, cols] = low

    row_t = lax.broadcasted_iota(jnp.int32, (columns, steps), 0) // p_count
    spread = (row_t == lax.broadcasted_iota(jnp.int32, (columns, steps), 1)).astype(BF16)
    same = (
        lax.broadcasted_iota(jnp.int32, (columns, columns), 0) % p_count
        == lax.broadcasted_iota(jnp.int32, (columns, columns), 1) % p_count
    )
    for part, mix in zip(split(noise[...]), (mix_h, mix_l)):
        rows = jnp.dot(spread, part, preferred_element_type=F32).astype(BF16)
        both = lax.dot_general(rows, spread, (((1,), (1,)), ((), ())), preferred_element_type=F32)
        mix[...] = jnp.where(same, both, 0.0).astype(BF16)

    zero_pad = jnp.zeros((span, par_rows), BF16)
    field[0:span, :] = jnp.zeros((span, par_rows), F32)
    for ref in (fe_h, fe_l, fo_h, fo_l):
        ref[0:span, :] = zero_pad
    for ref in (we_h, we_l, wo_h, wo_l):
        ref[columns:columns + span, :] = jnp.zeros((span, width), BF16)

    def first_splits(g, carry):
        slot = lax.rem(g, SLOTS)
        fetch(0, g, slot).wait()
        for i in range(LAGS):
            split_lag(slot, i, g * LAGS + i, 0)
        nxt = g + SLOTS
        fetch(nxt // groups, lax.rem(nxt, groups), slot).start()
        return carry

    lax.fori_loop(0, groups, first_splits, 0)

    for copy in gathers:
        copy.wait()
    for b in range(n_sens):
        field[span + b * own_cols:span + (b + 1) * own_cols, :] = gath[b].T
    fe_h[span:, :], fe_l[span:, :] = split(field[span:, :])
    fo_h[span:, :], fo_l[span:, :] = split(field[span - p_count:span - p_count + columns, :])

    def forward(chunk, g):
        start = span * g
        rows = columns - start
        left_h, left_l = [], []
        for i in range(LAGS):
            at = span - p_count * (i - i % 2)
            hi, lo = (fo_h, fo_l) if i % 2 else (fe_h, fe_l)
            left_h.append(hi[at:at + rows, :])
            left_l.append(lo[at:at + rows, :])
        lags = slice(g * LAGS * par_rows, (g + 1) * LAGS * par_rows)
        cols = slice(chunk * width, (chunk + 1) * width)
        term = dot3((jnp.concatenate(left_h, 1), jnp.concatenate(left_l, 1)), (k_h[lags, cols], k_l[lags, cols]))
        if g == 0:
            obs[chunk] = term
        else:
            obs[chunk, start:, :] += term

    def backward(chunk, g):
        start = span * g
        rows = columns - start
        left_h, left_l, right_h, right_l = [], [], [], []
        cols = slice(chunk * width, (chunk + 1) * width)
        for i in range(LAGS):
            at = start + p_count * (i - i % 2)
            hi, lo = (wo_h, wo_l) if i % 2 else (we_h, we_l)
            left_h.append(hi[at:at + rows, :])
            left_l.append(lo[at:at + rows, :])
            lag = slice((g * LAGS + i) * par_rows, (g * LAGS + i + 1) * par_rows)
            right_h.append(k_h[lag, cols])
            right_l.append(k_l[lag, cols])
        term = dot3(
            (jnp.concatenate(left_h, 1), jnp.concatenate(left_l, 1)),
            (jnp.concatenate(right_h, 1), jnp.concatenate(right_l, 1)), True)
        if g == 0 and chunk == 0:
            acc[...] = term
        else:
            acc[0:rows, :] += term

    def piece_of(index):
        return pl.ds(pl.multiple_of(index * piece, piece), piece)

    def scatter(chunk):
        copies = []
        for k in range(1, n_par):
            peer = lax.rem(par + k, n_par)
            copies.append(pltpu.make_async_remote_copy(
                src_ref=obs.at[chunk, piece_of(peer)], dst_ref=rs_buf.at[chunk, k],
                send_sem=rs_send.at[chunk, k], recv_sem=rs_recv.at[chunk, k],
                device_id={"par": peer}, device_id_type=MESH))
        for copy in copies:
            copy.start()
        return copies

    def reduce_and_spread(chunk, scatters):
        total = obs[chunk, piece_of(par)]
        for k, copy in enumerate(scatters, 1):
            copy.wait()
            total = total + rs_buf[chunk, k]
        full[chunk, piece_of(par)] = total
        copies = [
            pltpu.make_async_remote_copy(
                src_ref=full.at[chunk, piece_of(par)], dst_ref=full.at[chunk, piece_of(par)],
                send_sem=ag_send.at[chunk, k], recv_sem=ag_recv.at[chunk, k],
                device_id={"par": lax.rem(par + k, n_par)}, device_id_type=MESH)
            for k in range(1, n_par)
        ]
        for copy in copies:
            copy.start()
        return copies

    def weigh(chunk, spreads):
        for copy in spreads:
            copy.wait()
        mixed = dot3((mix_h[...], mix_l[...]), split(full[chunk]))
        mixed = mixed * weight[0:1, chunk * width:(chunk + 1) * width]
        we_h[0:columns, :], we_l[0:columns, :] = split(mixed)
        later = jnp.concatenate([mixed[p_count:], jnp.zeros((p_count, width), F32)], 0)
        wo_h[0:columns, :], wo_l[0:columns, :] = split(later)

    middle = 6 * groups // 16
    spreads = None
    scatters = None
    for chunk in range(chunks):
        for g in range(groups):
            if chunk > 0 and g == middle:
                spreads = reduce_and_spread(chunk - 1, scatters)
            if chunk + 1 < chunks:
                n = (chunk + 1) * groups + g
                fetch(chunk + 1, g, n % SLOTS).wait()
                for i in range(LAGS):
                    split_lag(n % SLOTS, i, g * LAGS + i, chunk + 1)
                nxt = n + SLOTS
                if nxt < chunks * groups:
                    fetch(nxt // groups, nxt % groups, nxt % SLOTS).start()
            forward(chunk, g)
        scatters = scatter(chunk)
    weigh(0, spreads)
    for g in range(groups):
        if g == middle:
            spreads = reduce_and_spread(1, scatters)
        backward(0, g)
    weigh(1, spreads)
    for g in range(groups):
        backward(1, g)

    def own_block(index):
        return pl.ds(pl.multiple_of(index * own_cols, own_cols), own_cols)

    finals = []
    for k in range(1, n_sens):
        peer = lax.rem(sens + k, n_sens)
        finals.append(pltpu.make_async_remote_copy(
            src_ref=acc.at[own_block(peer)], dst_ref=fin.at[k],
            send_sem=f_send.at[k], recv_sem=f_recv.at[k],
            device_id={"sens": peer}, device_id_type=MESH))
    for copy in finals:
        copy.start()
    total = acc[own_block(sens)]
    for k, copy in enumerate(finals, 1):
        copy.wait()
        total = total + fin[k]
    out[...] = total.T


def per_device(n_sens, n_par, probes, kern, noise, weight):
    steps, par_rows, sensors = kern.shape
    own_cols = probes.shape[1]
    columns = own_cols * n_sens
    p_count = columns // steps
    chunks = 2
    width = sensors // chunks
    span = LAGS * p_count
    piece = columns // n_par
    vmem, dma = pltpu.VMEM, pltpu.SemaphoreType.DMA
    in_vmem = pl.BlockSpec(memory_space=pltpu.VMEM)
    field = vmem((span + columns, par_rows), BF16)
    weighted = vmem((columns + span, width), BF16)
    whole = vmem((steps * par_rows, sensors), BF16)
    mix = vmem((columns, columns), BF16)
    return pl.pallas_call(
        functools.partial(kernel_body, n_sens, n_par, chunks),
        out_shape=jax.ShapeDtypeStruct(probes.shape, F32),
        in_specs=[in_vmem, pl.BlockSpec(memory_space=pl.ANY), in_vmem, in_vmem],
        out_specs=in_vmem,
        scratch_shapes=[
            vmem((n_sens, par_rows, own_cols), F32), vmem((span + columns, par_rows), F32),
            field, field, field, field,
            vmem((SLOTS, LAGS, par_rows, width), F32), whole, whole,
            vmem((chunks, columns, width), F32), vmem((chunks, n_par, piece, width), F32),
            vmem((chunks, columns, width), F32),
            weighted, weighted, weighted, weighted, mix, mix,
            vmem((columns, par_rows), F32), vmem((n_sens, own_cols, par_rows), F32),
            dma((SLOTS,)), dma((n_sens,)), dma((n_sens,)),
            dma((chunks, n_par)), dma((chunks, n_par)), dma((chunks, n_par)), dma((chunks, n_par)),
            dma((n_sens,)), dma((n_sens,)),
        ],
        compiler_params=pltpu.CompilerParams(
            collective_id=0, has_side_effects=True, vmem_limit_bytes=60 * 1024 * 1024),
    )(probes, kern, noise, weight.reshape(1, sensors))


def solution(mesh):
    placed = (P("par", "sens"), P(None, "par", "sens"), P(), P("sens"))
    body = functools.partial(per_device, mesh.shape["sens"], mesh.shape["par"])
    return jax.shard_map(body, mesh=mesh, in_specs=placed, out_specs=P("par", "sens"), check_vma=False)
```

```python
import functools

import jax
import jax.numpy as jnp
from jax import lax
from jax.experimental import pallas as pl
from jax.experimental.pallas import tpu as pltpu
from jax.sharding import PartitionSpec as P

MESH = pl.DeviceIdType.MESH
LAGS = 4
SLOTS = 8
F32 = jnp.float32
BF16 = jnp.bfloat16


def split(value):
    high = value.astype(BF16)
    return high, (value - high.astype(F32)).astype(BF16)


def dot3(left, right, transposed=False):
    side = 1 if transposed else 0
    (lh, ll), (rh, rl) = left, right
    return lax.dot_general(
        jnp.concatenate(lh + ll + lh, 1), jnp.concatenate(rh + rh + rl, side),
        dimension_numbers=(((1,), (side,)), ((), ())), preferred_element_type=F32)


def kernel_body(
    n_sens, n_par, chunks,
    probes, kern, noise, weight, out,
    gath, field, fe_h, fe_l, fo_h, fo_l, stage, k_h, k_l,
    obs, rs_buf, full, we_h, we_l, wo_h, wo_l, mix_h, mix_l, acc, fin,
    k_sem, g_send, g_recv, rs_send, rs_recv, ag_send, ag_recv, f_send, f_recv,
):
    steps, par_rows, sensors = kern.shape
    columns = acc.shape[0]
    p_count = columns // steps
    width = sensors // chunks
    groups = steps // LAGS
    span = LAGS * p_count
    own_cols = probes.shape[1]
    piece = columns // (2 * n_par)
    par, sens = lax.axis_index("par"), lax.axis_index("sens")

    def fetch(chunk, group, slot):
        return pltpu.make_async_copy(
            kern.at[pl.ds(group * LAGS, LAGS), :, pl.ds(pl.multiple_of(chunk * width, width), width)],
            stage.at[slot], k_sem.at[slot])

    for n in range(SLOTS):
        fetch(n // groups, n % groups, n % SLOTS).start()

    barrier = pltpu.get_barrier_semaphore()
    for k in range(1, n_par):
        pl.semaphore_signal(barrier, inc=1, device_id={"par": lax.rem(par + k, n_par)}, device_id_type=MESH)
    for k in range(1, n_sens):
        pl.semaphore_signal(barrier, inc=1, device_id={"sens": lax.rem(sens + k, n_sens)}, device_id_type=MESH)
    pl.semaphore_wait(barrier, n_par + n_sens - 2)

    twin = sens + 1 - 2 * lax.rem(sens, 2)
    across = lax.rem(sens + 2, n_sens)
    twin_across = lax.rem(twin + 2, n_sens)

    def to_sens(src, dst, k, device):
        return pltpu.make_async_remote_copy(
            src_ref=src, dst_ref=dst, send_sem=g_send.at[k], recv_sem=g_recv.at[k],
            device_id={"sens": device}, device_id_type=MESH)

    own_across = to_sens(probes, gath.at[sens], 1, across)
    own_twin = to_sens(probes, gath.at[sens], 0, twin)
    handed = to_sens(gath.at[across], gath.at[across], 2, twin)
    own_across.start()
    own_twin.start()
    gath[sens] = probes[...]

    def split_lag(slot, i, lag, chunk):
        high, low = split(stage[slot, i])
        rows = pl.ds(pl.multiple_of(lag * par_rows, par_rows), par_rows)
        cols = pl.ds(chunk * width, width)
        k_h[rows, cols] = high
        k_l[rows, cols] = low

    row_t = lax.broadcasted_iota(jnp.int32, (columns, steps), 0) // p_count
    spread = (row_t == lax.broadcasted_iota(jnp.int32, (columns, steps), 1)).astype(BF16)
    same = (
        lax.broadcasted_iota(jnp.int32, (columns, columns), 0) % p_count
        == lax.broadcasted_iota(jnp.int32, (columns, columns), 1) % p_count
    )
    for part, mix in zip(split(noise[...]), (mix_h, mix_l)):
        rows = jnp.dot(spread, part, preferred_element_type=F32).astype(BF16)
        both = lax.dot_general(rows, spread, (((1,), (1,)), ((), ())), preferred_element_type=F32)
        mix[...] = jnp.where(same, both, 0.0).astype(BF16)

    zero_pad = jnp.zeros((span, par_rows), BF16)
    field[0:span, :] = jnp.zeros((span, par_rows), F32)
    for ref in (fe_h, fe_l, fo_h, fo_l):
        ref[0:span, :] = zero_pad
    for ref in (we_h, we_l, wo_h, wo_l):
        ref[columns:columns + span, :] = jnp.zeros((span, width), BF16)

    def first_splits(g, carry):
        slot = lax.rem(g, SLOTS)
        fetch(0, g, slot).wait()
        for i in range(LAGS):
            split_lag(slot, i, g * LAGS + i, 0)
        nxt = g + SLOTS
        fetch(nxt // groups, lax.rem(nxt, groups), slot).start()
        return carry

    lax.fori_loop(0, 5 * groups // 8, first_splits, 0)
    own_across.wait_recv()
    handed.start()
    lax.fori_loop(5 * groups // 8, groups, first_splits, 0)
    own_across.wait_send()
    own_twin.wait()
    handed.wait()
    for b in range(n_sens):
        field[span + b * own_cols:span + (b + 1) * own_cols, :] = gath[b].T
    fe_h[span:, :], fe_l[span:, :] = split(field[span:, :])
    fo_h[span:, :], fo_l[span:, :] = split(field[span - p_count:span - p_count + columns, :])

    def forward(chunk, g):
        start = span * g
        rows = columns - start
        left_h, left_l = [], []
        for i in range(LAGS):
            at = span - p_count * (i - i % 2)
            hi, lo = (fo_h, fo_l) if i % 2 else (fe_h, fe_l)
            left_h.append(hi[at:at + rows, :])
            left_l.append(lo[at:at + rows, :])
        cols = slice(chunk * width, (chunk + 1) * width)
        term = None
        for at in range(0, LAGS, LAGS // 2):
            part = slice(at, at + LAGS // 2)
            lags = slice((g * LAGS + part.start) * par_rows, (g * LAGS + part.stop) * par_rows)
            product = dot3((left_h[part], left_l[part]), ([k_h[lags, cols]], [k_l[lags, cols]]))
            term = product if term is None else term + product
        if g == 0:
            obs[chunk] = term
        else:
            obs[chunk, start:, :] += term

    def backward(chunk, g):
        start = span * g
        rows = columns - start
        left_h, left_l, right_h, right_l = [], [], [], []
        cols = slice(chunk * width, (chunk + 1) * width)
        for i in range(LAGS):
            at = start + p_count * (i - i % 2)
            hi, lo = (wo_h, wo_l) if i % 2 else (we_h, we_l)
            left_h.append(hi[at:at + rows, :])
            left_l.append(lo[at:at + rows, :])
            lag = slice((g * LAGS + i) * par_rows, (g * LAGS + i + 1) * par_rows)
            right_h.append(k_h[lag, cols])
            right_l.append(k_l[lag, cols])
        term = None
        for at in range(0, LAGS, LAGS // 2):
            part = slice(at, at + LAGS // 2)
            product = dot3((left_h[part], left_l[part]), (right_h[part], right_l[part]), True)
            term = product if term is None else term + product
        if g == 0 and chunk == 0:
            acc[...] = term
        else:
            acc[0:rows, :] += term

    def piece_of(half, index):
        return pl.ds(pl.multiple_of(half * (columns // 2) + index * piece, piece), piece)

    def scatter(chunk, half):
        copies = []
        for k in range(1, n_par):
            peer = lax.rem(par + k, n_par)
            copies.append(pltpu.make_async_remote_copy(
                src_ref=obs.at[chunk, piece_of(half, peer)], dst_ref=rs_buf.at[chunk, half, k],
                send_sem=rs_send.at[chunk, half, k], recv_sem=rs_recv.at[chunk, half, k],
                device_id={"par": peer}, device_id_type=MESH))
        for copy in copies:
            copy.start()
        return copies

    def reduce_and_spread(chunk, half, scatters):
        total = obs[chunk, piece_of(half, par)]
        for k, copy in enumerate(scatters, 1):
            copy.wait()
            total = total + rs_buf[chunk, half, k]
        full[chunk, piece_of(half, par)] = total
        copies = [
            pltpu.make_async_remote_copy(
                src_ref=full.at[chunk, piece_of(half, par)], dst_ref=full.at[chunk, piece_of(half, par)],
                send_sem=ag_send.at[chunk, half, k], recv_sem=ag_recv.at[chunk, half, k],
                device_id={"par": lax.rem(par + k, n_par)}, device_id_type=MESH)
            for k in range(1, n_par)
        ]
        for copy in copies:
            copy.start()
        return copies

    def weigh(chunk, spreads):
        for copy in spreads:
            copy.wait()
        high, low = split(full[chunk])
        mixed = dot3(([mix_h[...]], [mix_l[...]]), ([high], [low]))
        mixed = mixed * weight[0:1, chunk * width:(chunk + 1) * width]
        we_h[0:columns, :], we_l[0:columns, :] = split(mixed)
        later = jnp.concatenate([mixed[p_count:], jnp.zeros((p_count, width), F32)], 0)
        wo_h[0:columns, :], wo_l[0:columns, :] = split(later)

    first_half = groups // 2
    turns = (groups // 8, 7 * groups // 16)
    sent = {}
    for chunk in range(chunks):
        for g in range(groups):
            for half, turn in enumerate(turns):
                if chunk > 0 and g == turn:
                    sent[half] = reduce_and_spread(chunk - 1, half, sent[half])
            if g == first_half:
                early = scatter(chunk, 0)
            if chunk + 1 < chunks:
                n = (chunk + 1) * groups + g
                fetch(chunk + 1, g, n % SLOTS).wait()
                for i in range(LAGS):
                    split_lag(n % SLOTS, i, g * LAGS + i, chunk + 1)
                nxt = n + SLOTS
                if nxt < chunks * groups:
                    fetch(nxt // groups, nxt % groups, nxt % SLOTS).start()
            forward(chunk, g)
        if chunk > 0:
            spreads = sent[0] + sent[1]
        sent = {0: early, 1: scatter(chunk, 1)}
    weigh(0, spreads)
    for g in range(groups):
        for half, turn in enumerate(turns):
            if g == turn:
                sent[half] = reduce_and_spread(1, half, sent[half])
        backward(0, g)
    weigh(1, sent[0] + sent[1])
    for g in range(groups):
        backward(1, g)

    def own_block(index):
        return pl.ds(pl.multiple_of(index * own_cols, own_cols), own_cols)

    def final(src, dst, k, device):
        return pltpu.make_async_remote_copy(
            src_ref=src, dst_ref=dst, send_sem=f_send.at[k], recv_sem=f_recv.at[k],
            device_id={"sens": device}, device_id_type=MESH)

    far = final(acc.at[own_block(twin_across)], fin.at[0], 0, twin)
    near = final(acc.at[own_block(twin)], fin.at[1], 1, twin)
    far.start()
    near.start()
    far.wait()
    fin[2] = acc[own_block(across)] + fin[0]
    last = final(fin.at[2], fin.at[3], 2, across)
    last.start()
    near.wait()
    total = acc[own_block(sens)] + fin[1]
    last.wait()
    out[...] = (total + fin[3]).T


def per_device(n_sens, n_par, probes, kern, noise, weight):
    steps, par_rows, sensors = kern.shape
    own_cols = probes.shape[1]
    columns = own_cols * n_sens
    p_count = columns // steps
    chunks = 2
    width = sensors // chunks
    span = LAGS * p_count
    piece = columns // (2 * n_par)
    vmem, dma = pltpu.VMEM, pltpu.SemaphoreType.DMA
    in_vmem = pl.BlockSpec(memory_space=pltpu.VMEM)
    field = vmem((span + columns, par_rows), BF16)
    weighted = vmem((columns + span, width), BF16)
    whole = vmem((steps * par_rows, sensors), BF16)
    mix = vmem((columns, columns), BF16)
    return pl.pallas_call(
        functools.partial(kernel_body, n_sens, n_par, chunks),
        out_shape=jax.ShapeDtypeStruct(probes.shape, F32),
        in_specs=[in_vmem, pl.BlockSpec(memory_space=pl.ANY), in_vmem, in_vmem],
        out_specs=in_vmem,
        scratch_shapes=[
            vmem((n_sens, par_rows, own_cols), F32), vmem((span + columns, par_rows), F32),
            field, field, field, field,
            vmem((SLOTS, LAGS, par_rows, width), F32), whole, whole,
            vmem((chunks, columns, width), F32), vmem((chunks, 2, n_par, piece, width), F32),
            vmem((chunks, columns, width), F32),
            weighted, weighted, weighted, weighted, mix, mix,
            vmem((columns, par_rows), F32), vmem((4, own_cols, par_rows), F32),
            dma((SLOTS,)), dma((n_sens,)), dma((n_sens,)),
            dma((chunks, 2, n_par)), dma((chunks, 2, n_par)), dma((chunks, 2, n_par)), dma((chunks, 2, n_par)),
            dma((n_sens,)), dma((n_sens,)),
        ],
        compiler_params=pltpu.CompilerParams(
            collective_id=0, has_side_effects=True, vmem_limit_bytes=60 * 1024 * 1024),
    )(probes, kern, noise, weight.reshape(1, sensors))


def solution(mesh):
    placed = (P("par", "sens"), P(None, "par", "sens"), P(), P("sens"))
    body = functools.partial(per_device, mesh.shape["sens"], mesh.shape["par"])
    return jax.shard_map(body, mesh=mesh, in_specs=placed, out_specs=P("par", "sens"), check_vma=False)
```
